32 devices in a mesh: ctx: 4 (over y, x), head: 4 (over z), fsdp: 2 (over core).
Axes of the slice: x: 2, y: 2, z: 4, core: 2. Of those that a mesh axis runs over, the one named last changes fastest.
Arguments:
- layer_input: bfloat16 [4096, 4096], P(('ctx', 'fsdp')), may hold values from -6 to 6
- query_act: bfloat16 [4096, 4096], P(('ctx', 'fsdp'), 'head'), may hold values from -6 to 6
- key_act: bfloat16 [4096, 4096], P(('ctx', 'fsdp'), 'head'), may hold values from -6 to 6
- out_grad: bfloat16 [4096, 4096], P(('ctx', 'fsdp'), 'head'), may hold values from -6 to 6
- value_weight: bfloat16 [4096, 4096], P('fsdp', 'head'), may hold values from -0.09375 to 0.09375
Outputs:
- query_grad: bfloat16 [4096, 4096], P(('ctx', 'fsdp'), 'head')
- key_grad: bfloat16 [4096, 4096], P(('ctx', 'fsdp'), 'head')
- input_grad: bfloat16 [4096, 4096], P(('ctx', 'fsdp'), 'head')
- weight_grad: float32 [4096, 4096], P(('ctx', 'fsdp'), 'head')
The draws below stay inside these ranges and needn't reach their ends.
All inputs are finite; a program needn't handle non-finite values.
Results may differ from the reference program's by a relative error of at most 0.018.
Values may be sent and summed in bfloat16 or wider, within the bound.
A program may use at most 128 MiB of HBM per device.

```python
import math
import jax
import jax.numpy as jnp
from jax import lax

D = 4096
HEADS = 32
HDIM = 128
TOK_DEV = 512
HD = 4096
TOKENS = 4096
N_HEAD = 4


def with_spikes(entries, key, source, target, blocks, factor):
    owner, partner = [(jnp.arange(entries.shape[position]) // (entries.shape[position] // blocks)).reshape([-1 if axis == position else 1 for axis in range(entries.ndim)]) for position in (source, target)]
    chosen = jax.random.permutation(key, blocks)[partner]
    strong = (owner == chosen) | (owner == (partner + blocks // 2) % blocks)
    return jnp.where(strong, factor * entries, entries)


def block_scale(key, dims, split, smallest, high):
    factor_of, own = 1.0, jax.random.fold_in(key, 6)
    for position, shards_of in split:
        draws = jnp.exp(jax.random.uniform(jax.random.fold_in(own, position), (shards_of,), jnp.float32, smallest / len(split), high / len(split)))
        factor_of = factor_of * jnp.repeat(draws, dims[position] // shards_of).reshape([-1 if axis == position else 1 for axis in range(len(dims))])
    return factor_of


def normal_values(stream_key, dims, spread, most, split=(), kind=jnp.bfloat16):
    values = spread * jax.random.normal(stream_key, dims, jnp.float32)
    if split:
        values = values * block_scale(stream_key, dims, split, -0.22, 0.18)
    return jnp.clip(values, -most, most).astype(kind)


def noise_with(own_key, extent, deviation, most, shards, heavy, held_as=jnp.bfloat16):
    result = deviation * jax.random.normal(own_key, extent, jnp.float32)
    if shards:
        result = result * block_scale(own_key, extent, shards, -0.22, 0.18)
    return jnp.clip(with_spikes(result, jax.random.fold_in(own_key, 3), *heavy), -most, most).astype(held_as)


def setup_inputs(seed: int = 0) -> dict:
    seeds = jax.random.split(jax.random.key(seed), 6)
    return {
        "layer_input": noise_with(seeds[0], (TOKENS, D), 1.0, 6.0, ((0, 8),), (0, 1, 8, 2.0)),
        "query_act": normal_values(seeds[1], (TOKENS, HD), 1.0, 6.0, ((0, 8), (1, 4))),
        "key_act": normal_values(seeds[2], (TOKENS, HD), 1.0, 6.0, ((0, 8), (1, 4))),
        "out_grad": normal_values(seeds[3], (TOKENS, HD), 1.0, 6.0, ((0, 8), (1, 4))),
        "value_weight": normal_values(seeds[4], (D, HD), D ** -0.5, 0.09375, ((0, 2), (1, 4))),
    }


def product(pattern, former, latter):
    return jnp.einsum(pattern, former, latter, precision=lax.Precision.HIGHEST)

def lowered(source):
    return lax.optimization_barrier(source.astype(jnp.bfloat16)).astype(jnp.float32)

def norm_grad(attended, grad_blk):
    inverse_rms = lax.rsqrt(lax.optimization_barrier(jnp.mean(attended * attended, axis=-1, keepdims=True)) + 1e-05)
    normed = attended * inverse_rms
    return inverse_rms * (grad_blk - normed * lax.optimization_barrier(jnp.mean(grad_blk * normed, axis=-1, keepdims=True)))

def block_backward(query_blk, key_blk, value_blk, grad_blk, state_prev, state_grad, causal):
    scores = product('thi,shi->hts', query_blk, key_blk)
    masked = lowered(jnp.where(causal[None], scores, 0.0))
    attended = product('hts,shj->thj', masked, value_blk) + product('thi,hij->thj', query_blk, state_prev)
    attn_grad = norm_grad(attended, grad_blk)
    attn_low = lowered(attn_grad)
    cross_terms = lowered(jnp.where(causal[None], product('thj,shj->hts', attn_low, value_blk), 0.0))
    query_part = product('hts,shi->thi', cross_terms, key_blk) + product('hij,thj->thi', state_prev, attn_grad)
    key_part = product('hts,thi->shi', cross_terms, query_blk) + product('hij,shj->shi', state_grad, value_blk)
    value_part = product('hts,thj->shj', masked, attn_low) + product('shi,hij->shj', key_blk, state_grad)
    local_grad = product('thi,thj->hij', query_blk, attn_grad)
    return (query_part, key_part, value_part, local_grad)

def reference(layer_input, query_act, key_act, out_grad, value_weight):
    blocks = TOKENS // TOK_DEV
    value_act = jnp.dot(layer_input, value_weight, preferred_element_type=jnp.float32).astype(jnp.bfloat16)

    def split_heads(source):
        return source.astype(jnp.float32).reshape(blocks, TOK_DEV, HEADS, HDIM)
    query_all = split_heads(query_act)
    key_all = split_heads(key_act)
    value_all = split_heads(value_act)
    grad_all = split_heads(out_grad)
    causal = jnp.tril(jnp.ones((TOK_DEV, TOK_DEV), dtype=bool))
    zero_state = jnp.zeros((HEADS, HDIM, HDIM), jnp.float32)

    def forward_step(carried, pieces):
        key_blk, value_blk = pieces
        update = product('shi,shj->hij', key_blk, value_blk)
        return (carried + update, carried)
    final_state, prior_states = lax.scan(forward_step, zero_state, (key_all, value_all))

    def backward_step(state_grad, pieces):
        query_blk, key_blk, value_blk, grad_blk, state_prev = pieces
        query_part, key_part, value_part, local_grad = block_backward(query_blk, key_blk, value_blk, grad_blk, state_prev, state_grad, causal)
        return (state_grad + local_grad, (query_part.astype(jnp.bfloat16), key_part.astype(jnp.bfloat16), value_part.astype(jnp.bfloat16)))
    unused, results = lax.scan(backward_step, zero_state, (query_all, key_all, value_all, grad_all, prior_states), reverse=True)
    query_grad = results[0].reshape(TOKENS, HEADS * HDIM)
    key_grad = results[1].reshape(TOKENS, HEADS * HDIM)
    value_grad = results[2].reshape(TOKENS, HEADS * HDIM)
    group_cols = HEADS * HDIM // N_HEAD
    input_sum = jnp.zeros((TOKENS, D), jnp.float32)
    for group in range(N_HEAD):
        grad_cols = value_grad[:, group * group_cols:(group + 1) * group_cols]
        weight_cols = value_weight[:, group * group_cols:(group + 1) * group_cols]
        partial_input = jnp.dot(grad_cols, weight_cols.T, preferred_element_type=jnp.float32)
        input_sum = input_sum + lowered(partial_input)
    input_grad = input_sum.astype(jnp.bfloat16)
    grad_scale = 1.0 / math.sqrt(TOKENS)

    def weight_step(running, pieces):
        input_blk, grad_blk = pieces
        partial_sum = jnp.dot(input_blk.T, grad_blk, preferred_element_type=jnp.float32) * grad_scale
        rounded = lax.optimization_barrier(partial_sum.astype(jnp.bfloat16))
        return (running + rounded.astype(jnp.float32), None)
    weight_grad, unused_too = lax.scan(weight_step, jnp.zeros((D, HEADS * HDIM), jnp.float32), (layer_input.reshape(blocks, TOK_DEV, D), value_grad.reshape(blocks, TOK_DEV, HEADS * HDIM)))
    return (query_grad, key_grad, input_grad, weight_grad)
```

```python
import math

import jax
import jax.numpy as jnp
from jax import lax
from jax.sharding import PartitionSpec as P

HDIM = 128
BF = jnp.bfloat16
F32 = jnp.float32


def dot(pattern, former, latter):
    return jnp.einsum(pattern, former, latter, preferred_element_type=F32)


def flip(array, axis, bit):
    size = lax.axis_size(axis)
    return lax.ppermute(array, axis, [(i, i ^ bit) for i in range(size)])


def bits_of(size):
    return [1 << k for k in range(size.bit_length() - 1)]


def scan_states(local_sum, later):
    ctx, core = lax.axis_index("ctx"), lax.axis_index("fsdp")
    low = local_sum.astype(BF)
    other = flip(low, "fsdp", 1).astype(F32)
    chip = local_sum + other
    half = local_sum.shape[0] // 2
    total = lax.dynamic_slice_in_dim(chip, core * half, half, 0)
    prefix = jnp.zeros_like(total)
    for bit in bits_of(lax.axis_size("ctx")):
        came = flip(total.astype(BF), "ctx", bit).astype(F32)
        mine_is_high = (ctx & bit) != 0
        use = jnp.logical_not(mine_is_high) if later else mine_is_high
        prefix = prefix + jnp.where(use, came, 0.0)
        total = total + came
    low = prefix.astype(BF)
    back = flip(low, "fsdp", 1)
    first = jnp.where(core == 0, low, back)
    second = jnp.where(core == 0, back, low)
    whole = jnp.concatenate([first, second], axis=0).astype(F32)
    use = (core == 0) if later else (core == 1)
    return (whole + jnp.where(use, other, 0.0)).astype(BF)


def line_sum(chunk_of, size, place):
    own = chunk_of(place)
    if size == 1:
        return own
    right = chunk_of(jnp.minimum(place + size - 1, size - 1))
    left = chunk_of(jnp.maximum(place - size + 1, 0))
    for step in range(size - 1):
        came_r = lax.ppermute(right.astype(BF), "head", [(z, z + 1) for z in range(step + 1)])
        came_l = lax.ppermute(
            left.astype(BF), "head", [(size - 1 - z, size - 2 - z) for z in range(step + 1)]
        )
        if step < size - 2:
            c_r = jnp.clip(size - 2 - step + place, 0, size - 1)
            c_l = jnp.clip(place - (size - 2 - step), 0, size - 1)
            right = came_r.astype(F32) + chunk_of(c_r)
            left = came_l.astype(F32) + chunk_of(c_l)
    return own + came_r.astype(F32) + came_l.astype(F32)


def halving(blocks, bits, ctx):
    size = blocks.shape[0]
    shape = blocks.shape[1:]
    names = bits_of(size)
    work = blocks.reshape((2,) * len(names) + shape)
    remaining = list(reversed(names))
    for bit in bits:
        at = remaining.index(bit)
        mine = (ctx & bit) != 0
        zero = lax.index_in_dim(work, 0, at, False)
        one = lax.index_in_dim(work, 1, at, False)
        send = jnp.where(mine, zero, one).astype(BF)
        keep = jnp.where(mine, one, zero)
        work = keep.astype(F32) + flip(send, "ctx", bit).astype(F32)
        remaining.pop(at)
    return work.reshape(shape)


def local(layer_input, query_act, key_act, out_grad, value_weight):
    tok, width = layer_input.shape
    ctx, core, head = (lax.axis_index(a) for a in ("ctx", "fsdp", "head"))
    n_ctx, n_head = lax.axis_size("ctx"), lax.axis_size("head")
    half_rows = value_weight.shape[0]
    weight_other = flip(value_weight, "fsdp", 1)
    x_mine = lax.dynamic_slice_in_dim(layer_input, core * half_rows, half_rows, 1)
    x_other = lax.dynamic_slice_in_dim(layer_input, (1 - core) * half_rows, half_rows, 1)
    value = (dot("td,de->te", x_mine, value_weight) + dot("td,de->te", x_other, weight_other)).astype(BF)
    heads = query_act.shape[1] // HDIM
    shape = (tok, heads, HDIM)
    q, k, v, g = (a.reshape(shape) for a in (query_act, key_act, value, out_grad))
    state = scan_states(dot("shi,shj->hij", k, v), False)
    causal = jnp.tril(jnp.ones((tok, tok), dtype=bool))[None]
    masked = jnp.where(causal, dot("thi,shi->hts", q, k), 0.0).astype(BF)
    attended = dot("hts,shj->thj", masked, v) + dot("thi,hij->thj", q, state)
    inv = lax.rsqrt(jnp.mean(attended * attended, axis=-1, keepdims=True) + 1e-05)
    normed = attended * inv
    gw = g.astype(F32)
    attn_low = (inv * (gw - normed * jnp.mean(gw * normed, axis=-1, keepdims=True))).astype(BF)
    grad_state = scan_states(dot("thi,thj->hij", q, attn_low), True)
    value_grad = (
        (dot("hts,thj->shj", masked, attn_low) + dot("shi,hij->shj", k, grad_state))
        .reshape(tok, -1)
        .astype(BF)
    )
    chunk = width // n_head
    per_half = half_rows // chunk if half_rows >= chunk else 0

    def weight_rows(index):
        if n_head == 1:
            first = jnp.where(core == 0, value_weight, weight_other)
            second = jnp.where(core == 0, weight_other, value_weight)
            return jnp.concatenate([first, second], axis=0)
        at = (index % per_half) * chunk
        mine = lax.dynamic_slice_in_dim(value_weight, at, chunk, 0)
        other = lax.dynamic_slice_in_dim(weight_other, at, chunk, 0)
        return jnp.where(index // per_half == core, mine, other)

    def chunk_of(index):
        return dot("te,de->td", value_grad, weight_rows(index))

    input_grad = line_sum(chunk_of, n_head, head).astype(BF)

    scale = 1.0 / math.sqrt(tok * n_ctx * 2)
    rows = width // (2 * n_ctx)
    x_blocks = layer_input.reshape(tok, n_ctx, 2, rows)

    def grad_rows(who):
        x_part = lax.dynamic_index_in_dim(x_blocks, who, 2, False)
        return dot("tcr,te->cre", x_part, value_grad) * scale

    came = flip(grad_rows(1 - core).astype(BF), "fsdp", 1)
    chip_sum = (grad_rows(core) + came.astype(F32)).astype(BF)
    cols = chip_sum.shape[2] // 2
    bits = bits_of(n_ctx)
    parts = [
        halving(chip_sum[:, :, :cols], bits, ctx),
        halving(chip_sum[:, :, cols:], bits[::-1], ctx),
    ]
    weight_grad = jnp.concatenate(parts, axis=1)

    cross = jnp.where(causal, dot("thj,shj->hts", attn_low, v), 0.0).astype(BF)
    query_grad = dot("hts,shi->thi", cross, k) + dot("hij,thj->thi", state, attn_low)
    key_grad = dot("hts,thi->shi", cross, q) + dot("hij,shj->shi", grad_state, v)
    query_grad = query_grad.reshape(tok, -1).astype(BF)
    key_grad = key_grad.reshape(tok, -1).astype(BF)
    return (query_grad, key_grad, input_grad, weight_grad)


def solution(mesh):
    spread = P(("ctx", "fsdp"), "head")
    in_specs = (P(("ctx", "fsdp"), None), spread, spread, spread, P("fsdp", "head"))
    return jax.shard_map(
        local, mesh=mesh, in_specs=in_specs, out_specs=(spread,) * 4, check_vma=False
    )
```
